32 devices in a mesh: ta: 4 (over y, x), gx: 2 (over core), gy: 4 (over z).
Axes of the slice: x: 2, y: 2, z: 4, core: 2. Of those that a mesh axis runs over, the one named last changes fastest.
Arguments:
- velocity: float32 [3, 4, 32, 64, 256], P(None, 'ta', 'gx', 'gy'), may hold values from -6 to 6
- pressure: float32 [4, 32, 64, 256], P('ta', 'gx', 'gy'), may hold values from -6 to 6
- forcing: float32 [3, 4, 32, 64, 256], P(None, 'ta', 'gx', 'gy'), may hold values from -6 to 6
- source: float32 [4, 32, 64, 256], P('ta', 'gx', 'gy'), may hold values from -6 to 6
- viscosity: float32 [3, 32, 64, 256], P(None, 'gx', 'gy'), may hold values from 0.05 to 0.5
Outputs:
- new_velocity: float32 [3, 4, 32, 64, 256], P(None, 'ta', 'gx', 'gy')
- new_pressure: float32 [4, 32, 64, 256], P('ta', 'gx', 'gy')
The draws below stay inside these ranges and needn't reach their ends.
All inputs are finite; a program needn't handle non-finite values.
Results may differ from the reference program's by a relative error of at most 0.00002.
Values sent between devices are 32-bit elements; how exact they have to be, the bound alone decides.
A program may use at most 64 MiB of HBM per device.

```python
import math
import jax
import jax.numpy as jnp

CZ = 256
SWEEPS = 2
NT = 4
NX = 32
NY = 64


def levels(stream_key, dims, shards, least, largest):
    gain, own = 1.0, jax.random.fold_in(stream_key, 6)
    for position, parts in shards:
        draws = jnp.exp(jax.random.uniform(jax.random.fold_in(own, position), (parts,), jnp.float32, least / len(shards), largest / len(shards)))
        gain = gain * jnp.repeat(draws, dims[position] // parts).reshape([-1 if axis == position else 1 for axis in range(len(dims))])
    return gain


def bell_draw(own_key, dims, spread, most, split=(), held_as=jnp.bfloat16):
    result = spread * jax.random.normal(own_key, dims, jnp.float32)
    if split:
        result = result * levels(own_key, dims, split, -0.22, 0.18)
    return jnp.clip(result, -most, most).astype(held_as)


def setup_inputs(seed: int = 0) -> dict:
    seeds = jax.random.split(jax.random.key(seed), 6)
    velocity = bell_draw(seeds[0], (3, NT, NX, NY, CZ), 1.0, 6.0, ((1, 4), (2, 2), (3, 4)), jnp.float32)
    pressure = bell_draw(seeds[1], (NT, NX, NY, CZ), 1.0, 6.0, ((0, 4), (1, 2), (2, 4)), jnp.float32)
    forcing = bell_draw(seeds[2], (3, NT, NX, NY, CZ), 1.0, 6.0, ((1, 4), (2, 2), (3, 4)), jnp.float32)
    source = bell_draw(seeds[3], (NT, NX, NY, CZ), 1.0, 6.0, ((0, 4), (1, 2), (2, 4)), jnp.float32)
    viscosity = jnp.clip(jnp.exp(math.log(0.5) - 2.3025851 * jax.random.uniform(seeds[4], (3, NX, NY, CZ), jnp.float32) ** levels(seeds[4], (3, NX, NY, CZ), ((1, 2), (2, 4)), -0.2, 0.2)), 0.05, 0.5)
    return {"velocity": velocity, "pressure": pressure, "forcing": forcing, "source": source, "viscosity": viscosity}


inverse_step = 1.0
relax_factor = 1.5
damping = 0.8


def gradient(field):
    return jnp.stack([jnp.roll(field, -1, -3) - field, jnp.roll(field, -1, -2) - field, jnp.roll(field, -1, -1) - field])


def divergence(flux):
    return (flux[0] - jnp.roll(flux[0], 1, -3)) + (flux[1] - jnp.roll(flux[1], 1, -2)) + (flux[2] - jnp.roll(flux[2], 1, -1))


def neighbours(field):
    total = jnp.roll(field, 1, -3) + jnp.roll(field, -1, -3)
    total = total + jnp.roll(field, 1, -2) + jnp.roll(field, -1, -2)
    return total + jnp.roll(field, 1, -1) + jnp.roll(field, -1, -1)


def diagonal_sum(coeff):
    return coeff[0] + jnp.roll(coeff[0], 1, -3) + coeff[1] + jnp.roll(coeff[1], 1, -2) + coeff[2] + jnp.roll(coeff[2], 1, -1)


def reference(velocity, pressure, forcing, source, viscosity):
    previous = jnp.concatenate([jnp.zeros_like(velocity[:, :1]), velocity[:, :-1]], axis=1)
    driven = forcing + inverse_step * previous
    visc = viscosity[:, None]
    momentum = driven - (inverse_step * velocity + visc * (6.0 * velocity - neighbours(velocity))) - gradient(pressure)
    coeff = 1.0 / (relax_factor * (inverse_step + 6.0 * visc))
    total = diagonal_sum(coeff)
    right = divergence(coeff * momentum) - (source - divergence(velocity))
    change = -damping * right / total
    for sweep in range(SWEEPS - 1):
        change = change - damping * (right - divergence(coeff * gradient(change))) / total
    new_velocity = velocity + coeff * (momentum - gradient(change))
    return new_velocity, pressure + change
```

```python
import functools

import jax
import jax.numpy as jnp
from jax import lax
from jax.experimental import pallas as pl
from jax.experimental.pallas import tpu as pltpu
from jax.sharding import PartitionSpec as P

relax_factor = 1.5
damping = 0.8
MESH = pl.DeviceIdType.MESH


def loop(lo, hi, body):
    def step(i, carry):
        body(i)
        return carry

    if hi > lo:
        lax.fori_loop(lo, hi, step, 0, unroll=2 if (hi - lo) % 2 == 0 else 1)


def row_index(f):
    return lax.broadcasted_iota(jnp.int32, f.shape, 0)


def y_next(f, row):
    n = f.shape[0]
    return jnp.where(row_index(f) == n - 1, row, pltpu.roll(f, n - 1, 0))


def y_last(f, row):
    return jnp.where(row_index(f) == 0, row, pltpu.roll(f, 1, 0))


def z_next(f):
    return pltpu.roll(f, f.shape[1] - 1, 1)


def z_last(f):
    return pltpu.roll(f, 1, 1)


def groups_of(lo, hi, size):
    return [(a, min(a + size, hi)) for a in range(lo, hi, size)]


def kernel(
    slabs, nx_parts, ny_parts, groups,
    vel, prs, frc, src, vis, out_v, out_p,
    V, Pr, F, S, Nu, C, W, SC, c1, c2, OV, OP,
    sE, rE, sI, rI, yu_s, yd_s, yu_r, yd_r, Ch, f_s, f_r,
    c1d_s, c1u_s, c1d_r, c1u_r, c2x_s, c2y_s, c2y_r,
    load_sem, out_sem, send_sem, recv_sem,
):
    _, nx, ny, nz = vel.shape
    parts = (ny - 4) // 4
    ta, gx, gy = lax.axis_index("ta"), lax.axis_index("gx"), lax.axis_index("gy")
    t_next, t_prev = lax.rem(ta + 1, slabs), lax.rem(ta + slabs - 1, slabs)
    has_next, has_prev = ta < slabs - 1, ta > 0
    xu, xd = lax.rem(gx + 1, nx_parts), lax.rem(gx + nx_parts - 1, nx_parts)
    yu, yd = lax.rem(gy + 1, ny_parts), lax.rem(gy + ny_parts - 1, ny_parts)

    loads = [
        pltpu.make_async_copy(vel, V.at[:, pl.ds(1, nx)], load_sem.at[0]),
        pltpu.make_async_copy(vis, Nu.at[:, pl.ds(1, nx)], load_sem.at[1]),
        pltpu.make_async_copy(prs, Pr.at[pl.ds(0, nx)], load_sem.at[2]),
        pltpu.make_async_copy(frc, F, load_sem.at[3]),
        pltpu.make_async_copy(src, S, load_sem.at[4]),
    ]
    for copy in loads:
        copy.start()

    barrier = pltpu.get_barrier_semaphore()
    for axis, index in (("gx", xu), ("gx", xd), ("gy", yu), ("gy", yd)):
        pl.semaphore_signal(barrier, inc=1, device_id={axis: index}, device_id_type=MESH)

    @pl.when(has_next)
    def _():
        pl.semaphore_signal(barrier, inc=1, device_id={"ta": t_next}, device_id_type=MESH)

    @pl.when(has_prev)
    def _():
        pl.semaphore_signal(barrier, inc=1, device_id={"ta": t_prev}, device_id_type=MESH)

    def remote(k, source, target, axis, index):
        return pltpu.make_async_remote_copy(
            src_ref=source, dst_ref=target, send_sem=send_sem.at[k], recv_sem=recv_sem.at[k],
            device_id={axis: index}, device_id_type=MESH,
        )

    vx_up = remote(0, V.at[:, nx], V.at[:, 0], "gx", xu)
    vx_dn = remote(1, V.at[:, 1], V.at[:, nx + 1], "gx", xd)
    px_dn = remote(2, Pr.at[0], Pr.at[nx], "gx", xd)
    nx_up = remote(3, Nu.at[0, nx], Nu.at[0, 0], "gx", xu)
    ry_up = remote(4, yu_s, yu_r, "gy", yu)
    ry_dn = remote(5, yd_s, yd_r, "gy", yd)
    fx_up = remote(6, W.at[0, nx], W.at[0, 0], "gx", xu)
    fy_up = remote(7, f_s, f_r, "gy", yu)
    cx_dn = remote(8, c1.at[1], c1.at[nx + 1], "gx", xd)
    cx_up = remote(9, c1.at[nx], c1.at[0], "gx", xu)
    cy_dn = remote(10, c1d_s, c1d_r, "gy", yd)
    cy_up = remote(11, c1u_s, c1u_r, "gy", yu)
    ex_dn = remote(12, c2x_s, c2.at[nx], "gx", xd)
    ey_dn = remote(13, c2y_s, c2y_r, "gy", yd)
    edge = remote(14, sE, rE, "ta", t_next)
    pieces = [
        remote(15 + k, sI.at[pl.ds(a, b - a)], rI.at[pl.ds(a, b - a)], "ta", t_next)
        for k, (a, b) in enumerate(groups)
    ]

    loads[0].wait()
    loads[1].wait()
    loads[2].wait()

    def pack_edges(x):
        for c in range(3):
            sE[c, x, 0:2] = V[c, x + 1, 0:2]
            sE[c, x, 2:4] = V[c, x + 1, ny - 2 : ny]
            yu_s[c, x] = V[c, x + 1, ny - 1 : ny]
            yd_s[c, x] = V[c, x + 1, 0:1]
        yu_s[3, x] = Nu[1, x + 1, ny - 1 : ny]
        yd_s[3, x] = Pr[x, 0:1]

    def pack_inner(x):
        for c in range(3):
            for p in range(parts):
                sI[x, p, c] = V[c, x + 1, 2 + 4 * p : 6 + 4 * p]

    loop(0, nx, pack_edges)
    pl.semaphore_wait(barrier, 4 + has_next.astype(jnp.int32) + has_prev.astype(jnp.int32))

    @pl.when(has_next)
    def _():
        edge.start()

    for copy in (ry_up, ry_dn, vx_up, vx_dn, px_dn, nx_up):
        copy.start()

    loop(0, nx, pack_inner)

    @pl.when(has_next)
    def _():
        for copy in pieces:
            copy.start()

    def coeff_of(nu):
        return 1.0 / (relax_factor * (1.0 + 6.0 * nu))

    loads[3].wait()
    loads[4].wait()
    for copy in (vx_up, vx_dn, px_dn, nx_up, ry_up, ry_dn):
        copy.wait_recv()
    C[0, 0] = coeff_of(Nu[0, 0])

    def prepare(x):
        e = x + 1
        below = coeff_of(yu_r[3, x])
        Ch[x] = below
        coeff = [coeff_of(Nu[c, e]) for c in range(3)]
        for c in range(3):
            C[c, e] = coeff[c]
        total = coeff[0] + C[0, x] + coeff[1] + y_last(coeff[1], below) + coeff[2] + z_last(coeff[2])
        SC[x] = damping / total
        press = Pr[x]
        grads = (Pr[x + 1] - press, y_next(press, yd_r[3, x]) - press, z_next(press) - press)
        for c in range(3):
            v = V[c, e]
            near = V[c, e - 1] + V[c, e + 1] + y_last(v, yu_r[c, x]) + y_next(v, yd_r[c, x])
            near = near + z_last(v) + z_next(v)
            momentum = F[c, x] - (v + Nu[c, e] * (6.0 * v - near)) - grads[c]
            W[c, e] = v + coeff[c] * momentum

    loop(0, nx, prepare)

    def add_edges(x):
        for c in range(3):
            for s, t in ((0, 0), (2, ny - 2)):
                W[c, x + 1, t : t + 2] = (
                    W[c, x + 1, t : t + 2] + C[c, x + 1, t : t + 2] * rE[c, x, s : s + 2]
                )

    def add_inner(x):
        for c in range(3):
            for p in range(parts):
                t = 2 + 4 * p
                W[c, x + 1, t : t + 4] = W[c, x + 1, t : t + 4] + C[c, x + 1, t : t + 4] * rI[x, p, c]

    def arrive(k):
        @pl.when(has_prev)
        def _():
            pieces[k].wait_recv()
            loop(*groups[k], add_inner)

    @pl.when(has_prev)
    def _():
        edge.wait_recv()
        loop(0, nx, add_edges)

    def pack_flux(x):
        f_s[x] = W[1, x + 1, ny - 1 : ny]

    loop(0, nx, pack_flux)
    fy_up.start()
    arrive(0)
    arrive(1)
    fx_up.start()
    fx_up.wait_recv()
    fy_up.wait_recv()

    def sweep_one(x):
        e = x + 1
        w1, w2 = W[1, e], W[2, e]
        div = (W[0, e] - W[0, x]) + (w1 - y_last(w1, f_r[x])) + (w2 - z_last(w2))
        return SC[x] * (S[x] - div)

    def first_edges(x):
        change = sweep_one(x)
        c1[x + 1] = change
        c1d_s[x] = change[0:1]
        c1u_s[x] = change[ny - 1 : ny]

    loop(0, nx, first_edges)
    for copy in (cy_dn, cy_up, cx_dn, cx_up):
        copy.start()
    for copy in (cx_dn, cx_up, cy_dn, cy_up):
        copy.wait_recv()

    def sweep_two(x):
        e = x + 1
        here = c1[e]
        w0 = W[0, e] - C[0, e] * (c1[e + 1] - here)
        w0_last = W[0, x] - C[0, x] * (here - c1[x])
        w1 = W[1, e] - C[1, e] * (y_next(here, c1d_r[x]) - here)
        row = f_r[x] - Ch[x] * (here[0:1] - c1u_r[x])
        w2 = W[2, e] - C[2, e] * (z_next(here) - here)
        div = (w0 - w0_last) + (w1 - y_last(w1, row)) + (w2 - z_last(w2))
        return here + SC[x] * (S[x] - div)

    c2x_s[...] = sweep_two(0)

    def second_edges(x):
        c2y_s[x] = sweep_two(x)[0:1]

    loop(0, nx, second_edges)
    ey_dn.start()
    ex_dn.start()

    for copy in (cx_dn, cx_up):
        copy.wait_send()

    def first(x):
        c1[x + 1] = sweep_one(x)

    def second(x):
        c2[x] = sweep_two(x)

    done = 0
    for k in range(2, len(groups)):
        arrive(k)
        stop = groups[k][1] if k < len(groups) - 1 else nx
        loop(done, stop, first)
        loop(max(done - 1, 0), stop - 1 if stop < nx else nx, second)
        done = stop

    ex_dn.wait_recv()
    ey_dn.wait_recv()

    def finish(x):
        e = x + 1
        here = c2[x]
        OP[x] = Pr[x] + here
        OV[0, x] = W[0, e] - C[0, e] * (c2[x + 1] - here)
        OV[1, x] = W[1, e] - C[1, e] * (y_next(here, c2y_r[x]) - here)
        OV[2, x] = W[2, e] - C[2, e] * (z_next(here) - here)

    stores = []
    for k, (a, b) in enumerate(groups_of(0, nx, -(-nx // 4))):
        loop(a, b, finish)
        part = pl.ds(a, b - a)
        stores.append(pltpu.make_async_copy(OV.at[:, part], out_v.at[:, part], out_sem.at[2 * k]))
        stores.append(pltpu.make_async_copy(OP.at[part], out_p.at[part], out_sem.at[2 * k + 1]))
        for copy in stores[-2:]:
            copy.start()

    @pl.when(has_next)
    def _():
        edge.wait_send()
        for copy in pieces:
            copy.wait_send()

    for copy in (vx_up, vx_dn, px_dn, nx_up, ry_up, ry_dn, fx_up, fy_up, cy_dn, cy_up, ex_dn, ey_dn):
        copy.wait_send()
    for copy in stores:
        copy.wait()


def body(counts, velocity, pressure, forcing, source, viscosity):
    _, steps, nx, ny, nz = velocity.shape
    assert steps == 1 and nx >= 5 and ny >= 8 and ny % 4 == 0
    groups = [(0, 2), (nx - 2, nx)] + groups_of(2, nx - 2, 4)
    parts = (ny - 4) // 4
    vmem = lambda *shape: pltpu.VMEM(shape, jnp.float32)
    rows = lambda *lead: vmem(*lead, nx, 1, nz)
    any_space = pl.BlockSpec(memory_space=pl.ANY)
    out_v, out_p = pl.pallas_call(
        functools.partial(kernel, *counts, groups),
        out_shape=(
            jax.ShapeDtypeStruct((3, nx, ny, nz), jnp.float32),
            jax.ShapeDtypeStruct((nx, ny, nz), jnp.float32),
        ),
        in_specs=[any_space] * 5,
        out_specs=(any_space, any_space),
        scratch_shapes=[
            vmem(3, nx + 2, ny, nz), vmem(nx + 1, ny, nz), vmem(3, nx, ny, nz), vmem(nx, ny, nz),
            vmem(3, nx + 1, ny, nz), vmem(3, nx + 1, ny, nz), vmem(3, nx + 1, ny, nz),
            vmem(nx, ny, nz), vmem(nx + 2, ny, nz), vmem(nx + 1, ny, nz),
            vmem(3, nx, ny, nz), vmem(nx, ny, nz),
            vmem(3, nx, 4, nz), vmem(3, nx, 4, nz),
            vmem(nx, parts, 3, 4, nz), vmem(nx, parts, 3, 4, nz),
            rows(4), rows(4), rows(4), rows(4), rows(), rows(), rows(),
            rows(), rows(), rows(), rows(), vmem(ny, nz), rows(), rows(),
            pltpu.SemaphoreType.DMA((5,)),
            pltpu.SemaphoreType.DMA((8,)),
            pltpu.SemaphoreType.DMA((15 + len(groups),)),
            pltpu.SemaphoreType.DMA((15 + len(groups),)),
        ],
        compiler_params=pltpu.CompilerParams(
            collective_id=0, has_side_effects=True, vmem_limit_bytes=48 << 20
        ),
        name="smoother",
    )(velocity[:, 0], pressure[0], forcing[:, 0], source[0], viscosity)
    return out_v[:, None], out_p[None]


def solution(mesh):
    placed = (
        P(None, "ta", "gx", "gy", None),
        P("ta", "gx", "gy", None),
        P(None, "ta", "gx", "gy", None),
        P("ta", "gx", "gy", None),
        P(None, "gx", "gy", None),
    )
    counts = tuple(mesh.shape[axis] for axis in ("ta", "gx", "gy"))
    return jax.shard_map(
        functools.partial(body, counts),
        mesh=mesh,
        in_specs=placed,
        out_specs=(P(None, "ta", "gx", "gy", None), P("ta", "gx", "gy", None)),
        check_vma=False,
    )
```

```python
import functools

import jax
import jax.numpy as jnp
from jax import lax
from jax.experimental import pallas as pl
from jax.experimental.pallas import tpu as pltpu
from jax.sharding import PartitionSpec as P

relax_factor = 1.5
damping = 0.8
MESH = pl.DeviceIdType.MESH


def loop(lo, hi, body):
    def step(i, carry):
        body(i)
        return carry

    if hi > lo:
        lax.fori_loop(lo, hi, step, 0, unroll=hi - lo)


def row_index(f):
    return lax.broadcasted_iota(jnp.int32, f.shape, 0)


def y_next(f, row):
    n = f.shape[0]
    return jnp.where(row_index(f) == n - 1, row, pltpu.roll(f, n - 1, 0))


def y_last(f, row):
    return jnp.where(row_index(f) == 0, row, pltpu.roll(f, 1, 0))


def z_next(f):
    return pltpu.roll(f, f.shape[1] - 1, 1)


def z_last(f):
    return pltpu.roll(f, 1, 1)


def groups_of(lo, hi, size):
    return [(a, min(a + size, hi)) for a in range(lo, hi, size)]


def kernel(
    slabs, nx_parts, ny_parts, groups,
    vel, prs, frc, src, vis, out_v, out_p,
    V, Pr, F, S, Nu, C, W, SC, c1, c2, OV, OP,
    sE, rE, sI, rI, yu_s, yd_s, yu_r, yd_r, Ch, f_s, f_r, Fh, rP,
    c1d_s, c1u_s, c1d_r, c1u_r, c2x_s, c2y_s, c2y_r,
    load_sem, out_sem, send_sem, recv_sem,
):
    _, nx, ny, nz = vel.shape
    parts = (ny - 4) // 4
    ta, gx, gy = lax.axis_index("ta"), lax.axis_index("gx"), lax.axis_index("gy")
    t_next, t_prev = lax.rem(ta + 1, slabs), lax.rem(ta + slabs - 1, slabs)
    has_next, has_prev = ta < slabs - 1, ta > 0
    xu, xd = lax.rem(gx + 1, nx_parts), lax.rem(gx + nx_parts - 1, nx_parts)
    yu, yd = lax.rem(gy + 1, ny_parts), lax.rem(gy + ny_parts - 1, ny_parts)

    loads = [
        pltpu.make_async_copy(vel, V.at[:, pl.ds(1, nx)], load_sem.at[0]),
        pltpu.make_async_copy(vis, Nu.at[:, pl.ds(1, nx)], load_sem.at[1]),
        pltpu.make_async_copy(prs, Pr.at[pl.ds(0, nx)], load_sem.at[2]),
        pltpu.make_async_copy(frc, F, load_sem.at[3]),
        pltpu.make_async_copy(src, S, load_sem.at[4]),
    ]
    for copy in loads:
        copy.start()

    barrier = pltpu.get_barrier_semaphore()
    for axis, index in (("gx", xu), ("gx", xd), ("gy", yu), ("gy", yd)):
        pl.semaphore_signal(barrier, inc=1, device_id={axis: index}, device_id_type=MESH)

    @pl.when(has_next)
    def _():
        pl.semaphore_signal(barrier, inc=1, device_id={"ta": t_next}, device_id_type=MESH)

    @pl.when(has_prev)
    def _():
        pl.semaphore_signal(barrier, inc=1, device_id={"ta": t_prev}, device_id_type=MESH)

    def remote(k, source, target, axis, index):
        return pltpu.make_async_remote_copy(
            src_ref=source, dst_ref=target, send_sem=send_sem.at[k], recv_sem=recv_sem.at[k],
            device_id={axis: index}, device_id_type=MESH,
        )

    vx_up = remote(0, V.at[:, nx], V.at[:, 0], "gx", xu)
    vx_dn = remote(1, V.at[:, 1], V.at[:, nx + 1], "gx", xd)
    px_dn = remote(2, Pr.at[0], Pr.at[nx], "gx", xd)
    nx_up = remote(3, Nu.at[0, nx], Nu.at[0, 0], "gx", xu)
    ry_up = remote(4, yu_s, yu_r, "gy", yu)
    ry_dn = remote(5, yd_s, yd_r, "gy", yd)
    fx_up = remote(6, W.at[0, nx], W.at[0, 0], "gx", xu)
    fy_up = remote(7, f_s, f_r, "gy", yu)
    cx_dn = remote(8, c1.at[1], c1.at[nx + 1], "gx", xd)
    cx_up = remote(9, c1.at[nx], c1.at[0], "gx", xu)
    cy_dn = remote(10, c1d_s, c1d_r, "gy", yd)
    cy_up = remote(11, c1u_s, c1u_r, "gy", yu)
    ex_dn = remote(12, c2x_s, c2.at[nx], "gx", xd)
    ey_dn = remote(13, c2y_s, c2y_r, "gy", yd)
    edge = remote(14, sE, rE, "ta", t_next)
    border = remote(15, yu_r.at[1], rP, "ta", t_next)
    pieces = [
        remote(16 + k, sI.at[pl.ds(a, b - a)], rI.at[pl.ds(a, b - a)], "ta", t_next)
        for k, (a, b) in enumerate(groups)
    ]

    def pack_edges(x):
        for c in range(3):
            sE[c, x, 0:2] = V[c, x + 1, 0:2]
            sE[c, x, 2:4] = V[c, x + 1, ny - 2 : ny]

    def pack_rows(x):
        for c in range(3):
            yu_s[c, x] = V[c, x + 1, ny - 1 : ny]
            yd_s[c, x] = V[c, x + 1, 0:1]
        yu_s[3, x] = Nu[1, x + 1, ny - 1 : ny]
        yd_s[3, x] = Pr[x, 0:1]

    def pack_inner(x):
        for c in range(3):
            for p in range(parts):
                sI[x, p, c] = V[c, x + 1, 2 + 4 * p : 6 + 4 * p]

    loads[0].wait()
    loop(0, nx, pack_edges)
    pl.semaphore_wait(barrier, 4 + has_next.astype(jnp.int32) + has_prev.astype(jnp.int32))

    @pl.when(has_next)
    def _():
        edge.start()

    loads[1].wait()
    loads[2].wait()
    loop(0, nx, pack_rows)
    for copy in (ry_up, ry_dn, vx_up, vx_dn, px_dn, nx_up):
        copy.start()

    loop(0, nx, pack_inner)

    @pl.when(has_next)
    def _():
        for copy in pieces[:2]:
            copy.start()

    ry_up.wait_recv()

    @pl.when(has_next)
    def _():
        for copy in (border, *pieces[2:]):
            copy.start()

    def coeff_of(nu):
        return 1.0 / (relax_factor * (1.0 + 6.0 * nu))

    loads[3].wait()
    loads[4].wait()
    for copy in (vx_up, vx_dn, px_dn, nx_up, ry_dn):
        copy.wait_recv()
    C[0, 0] = coeff_of(Nu[0, 0])

    def prepare(x):
        e = x + 1
        below = coeff_of(yu_r[3, x])
        Ch[x] = below
        coeff = [coeff_of(Nu[c, e]) for c in range(3)]
        for c in range(3):
            C[c, e] = coeff[c]
        total = coeff[0] + C[0, x] + coeff[1] + y_last(coeff[1], below) + coeff[2] + z_last(coeff[2])
        SC[x] = damping / total
        press = Pr[x]
        grads = (Pr[x + 1] - press, y_next(press, yd_r[3, x]) - press, z_next(press) - press)
        for c in range(3):
            v = V[c, e]
            near = V[c, e - 1] + V[c, e + 1] + y_last(v, yu_r[c, x]) + y_next(v, yd_r[c, x])
            near = near + z_last(v) + z_next(v)
            momentum = F[c, x] - (v + Nu[c, e] * (6.0 * v - near)) - grads[c]
            W[c, e] = v + coeff[c] * momentum
        f_s[x] = W[1, e, ny - 1 : ny]

    loop(0, nx, prepare)
    fy_up.start()

    def add_edges(x):
        for c in range(3):
            for s, t in ((0, 0), (2, ny - 2)):
                W[c, x + 1, t : t + 2] = (
                    W[c, x + 1, t : t + 2] + C[c, x + 1, t : t + 2] * rE[c, x, s : s + 2]
                )

    def add_inner(x):
        for c in range(3):
            for p in range(parts):
                t = 2 + 4 * p
                W[c, x + 1, t : t + 4] = W[c, x + 1, t : t + 4] + C[c, x + 1, t : t + 4] * rI[x, p, c]

    def arrive(k):
        @pl.when(has_prev)
        def _():
            pieces[k].wait_recv()
            loop(*groups[k], add_inner)

    @pl.when(has_prev)
    def _():
        edge.wait_recv()
        loop(0, nx, add_edges)

    arrive(0)
    arrive(1)
    fx_up.start()
    fy_up.wait_recv()

    @pl.when(has_prev)
    def _():
        border.wait_recv()
        Fh[...] = f_r[...] + Ch[...] * rP[...]

    @pl.when(jnp.logical_not(has_prev))
    def _():
        Fh[...] = f_r[...]

    fx_up.wait_recv()

    def sweep_one(x):
        e = x + 1
        w1, w2 = W[1, e], W[2, e]
        div = (W[0, e] - W[0, x]) + (w1 - y_last(w1, Fh[x])) + (w2 - z_last(w2))
        return SC[x] * (S[x] - div)

    def first_edges(x):
        change = sweep_one(x)
        c1[x + 1] = change
        c1d_s[x] = change[0:1]
        c1u_s[x] = change[ny - 1 : ny]

    loop(0, nx, first_edges)
    for copy in (cy_dn, cy_up, cx_dn, cx_up):
        copy.start()
    for copy in (cx_dn, cx_up, cy_dn, cy_up):
        copy.wait_recv()

    def sweep_two(x):
        e = x + 1
        here = c1[e]
        w0 = W[0, e] - C[0, e] * (c1[e + 1] - here)
        w0_last = W[0, x] - C[0, x] * (here - c1[x])
        w1 = W[1, e] - C[1, e] * (y_next(here, c1d_r[x]) - here)
        row = Fh[x] - Ch[x] * (here[0:1] - c1u_r[x])
        w2 = W[2, e] - C[2, e] * (z_next(here) - here)
        div = (w0 - w0_last) + (w1 - y_last(w1, row)) + (w2 - z_last(w2))
        return here + SC[x] * (S[x] - div)

    c2x_s[...] = sweep_two(0)

    def second_edges(x):
        c2y_s[x] = sweep_two(x)[0:1]

    loop(0, nx, second_edges)
    ey_dn.start()
    ex_dn.start()

    for copy in (cx_dn, cx_up):
        copy.wait_send()

    def first(x):
        c1[x + 1] = sweep_one(x)

    def second(x):
        c2[x] = sweep_two(x)

    def finish(x):
        e = x + 1
        here = c2[x]
        OP[x] = Pr[x] + here
        OV[0, x] = W[0, e] - C[0, e] * (c2[x + 1] - here)
        OV[1, x] = W[1, e] - C[1, e] * (y_next(here, c2y_r[x]) - here)
        OV[2, x] = W[2, e] - C[2, e] * (z_next(here) - here)

    stores = []

    def emit(a, b):
        k = len(stores)
        loop(a, b, finish)
        part = pl.ds(a, b - a)
        stores.append(pltpu.make_async_copy(OV.at[:, part], out_v.at[:, part], out_sem.at[k]))
        stores.append(pltpu.make_async_copy(OP.at[part], out_p.at[part], out_sem.at[k + 1]))
        for copy in stores[-2:]:
            copy.start()

    done = 0
    for k in range(2, len(groups)):
        last = k == len(groups) - 1
        if last:
            ex_dn.wait_recv()
            ey_dn.wait_recv()
            ready = done - 2
            emit(0, ready)
        arrive(k)
        stop = nx if last else groups[k][1]
        loop(done, stop, first)
        loop(max(done - 1, 0), nx if last else stop - 1, second)
        done = stop
    emit(ready, nx)

    @pl.when(has_next)
    def _():
        edge.wait_send()
        border.wait_send()
        for copy in pieces:
            copy.wait_send()

    for copy in (vx_up, vx_dn, px_dn, nx_up, ry_up, ry_dn, fx_up, fy_up, cy_dn, cy_up, ex_dn, ey_dn):
        copy.wait_send()
    for copy in stores:
        copy.wait()


def place(from_v, from_p, out_v, out_p, sem):
    copies = [
        pltpu.make_async_copy(from_v.at[c], out_v.at[c], sem.at[c]) for c in range(3)
    ] + [pltpu.make_async_copy(from_p, out_p, sem.at[3])]
    for copy in copies:
        copy.start()
    for copy in copies:
        copy.wait()


def body(counts, velocity, pressure, forcing, source, viscosity):
    _, steps, nx, ny, nz = velocity.shape
    assert steps == 1 and nx >= 8 and ny >= 8 and ny % 4 == 0
    groups = [(0, 2), (nx - 2, nx)] + groups_of(2, nx - 4, 5) + [(nx - 4, nx - 2)]
    parts = (ny - 4) // 4
    vmem = lambda *shape: pltpu.VMEM(shape, jnp.float32)
    rows = lambda *lead: vmem(*lead, nx, 1, nz)
    any_space = pl.BlockSpec(memory_space=pl.ANY)
    out_v, out_p = pl.pallas_call(
        functools.partial(kernel, *counts, groups),
        out_shape=(
            jax.ShapeDtypeStruct((3, nx, ny, nz), jnp.float32),
            jax.ShapeDtypeStruct((nx, ny, nz), jnp.float32),
        ),
        in_specs=[any_space] * 5,
        out_specs=(any_space, any_space),
        scratch_shapes=[
            vmem(3, nx + 2, ny, nz), vmem(nx + 1, ny, nz), vmem(3, nx, ny, nz), vmem(nx, ny, nz),
            vmem(3, nx + 1, ny, nz), vmem(3, nx + 1, ny, nz), vmem(3, nx + 1, ny, nz),
            vmem(nx, ny, nz), vmem(nx + 2, ny, nz), vmem(nx + 1, ny, nz),
            vmem(3, nx, ny, nz), vmem(nx, ny, nz),
            vmem(3, nx, 4, nz), vmem(3, nx, 4, nz),
            vmem(nx, parts, 3, 4, nz), vmem(nx, parts, 3, 4, nz),
            rows(4), rows(4), rows(4), rows(4), rows(), rows(), rows(), rows(), rows(),
            rows(), rows(), rows(), rows(), vmem(ny, nz), rows(), rows(),
            pltpu.SemaphoreType.DMA((5,)),
            pltpu.SemaphoreType.DMA((4,)),
            pltpu.SemaphoreType.DMA((16 + len(groups),)),
            pltpu.SemaphoreType.DMA((16 + len(groups),)),
        ],
        compiler_params=pltpu.CompilerParams(
            collective_id=0, has_side_effects=True, vmem_limit_bytes=48 << 20
        ),
        name="smoother",
    )(*(pltpu.with_memory_space_constraint(a, pltpu.HBM) for a in (velocity[:, 0], pressure[0], forcing[:, 0], source[0], viscosity)))
    out_v, out_p = pl.pallas_call(
        place,
        out_shape=(
            jax.ShapeDtypeStruct(out_v.shape, jnp.float32),
            jax.ShapeDtypeStruct(out_p.shape, jnp.float32),
        ),
        in_specs=[any_space] * 2,
        out_specs=(any_space, any_space),
        scratch_shapes=[pltpu.SemaphoreType.DMA((4,))],
        compiler_params=pltpu.CompilerParams(vmem_limit_bytes=1 << 20),
        name="place",
    )(out_v, out_p)
    return out_v[:, None], out_p[None]


def solution(mesh):
    placed = (
        P(None, "ta", "gx", "gy", None),
        P("ta", "gx", "gy", None),
        P(None, "ta", "gx", "gy", None),
        P("ta", "gx", "gy", None),
        P(None, "gx", "gy", None),
    )
    counts = tuple(mesh.shape[axis] for axis in ("ta", "gx", "gy"))
    return jax.shard_map(
        functools.partial(body, counts),
        mesh=mesh,
        in_specs=placed,
        out_specs=(P(None, "ta", "gx", "gy", None), P("ta", "gx", "gy", None)),
        check_vma=False,
    )
```

```python
import functools

import jax
import jax.numpy as jnp
from jax import lax
from jax.experimental import pallas as pl
from jax.experimental.pallas import tpu as pltpu
from jax.sharding import PartitionSpec as P

relax_factor = 1.5
damping = 0.8
MESH = pl.DeviceIdType.MESH


def loop(lo, hi, body):
    def step(i, carry):
        body(i)
        return carry

    if hi > lo:
        lax.fori_loop(lo, hi, step, 0, unroll=hi - lo)


def row_index(f):
    return lax.broadcasted_iota(jnp.int32, f.shape, 0)


def y_next(f, row):
    n = f.shape[0]
    return jnp.where(row_index(f) == n - 1, row, pltpu.roll(f, n - 1, 0))


def y_last(f, row):
    return jnp.where(row_index(f) == 0, row, pltpu.roll(f, 1, 0))


def z_next(f):
    return pltpu.roll(f, f.shape[1] - 1, 1)


def z_last(f):
    return pltpu.roll(f, 1, 1)


def groups_of(lo, hi, size):
    return [(a, min(a + size, hi)) for a in range(lo, hi, size)]


def kernel(
    slabs, nx_parts, ny_parts, groups,
    vel, prs, frc, src, vis, out_v, out_p,
    V, Pr, F, S, Nu, C, W, SC, c1, c2,
    sE, rE, sI, rI, yu_s, yd_s, yu_r, yd_r, Ch, f_s, f_r, Fh, rP, rX, fe_r,
    c1d_s, c1u_s, c1d_r, c1u_r, c2x_s, c2y_s, c2y_r,
    load_sem, send_sem, recv_sem,
):
    _, nx, ny, nz = vel.shape
    parts = (ny - 4) // 4
    ta, gx, gy = lax.axis_index("ta"), lax.axis_index("gx"), lax.axis_index("gy")
    t_next, t_prev = lax.rem(ta + 1, slabs), lax.rem(ta + slabs - 1, slabs)
    has_next, has_prev = ta < slabs - 1, ta > 0
    xu, xd = lax.rem(gx + 1, nx_parts), lax.rem(gx + nx_parts - 1, nx_parts)
    yu, yd = lax.rem(gy + 1, ny_parts), lax.rem(gy + ny_parts - 1, ny_parts)

    loads = [
        pltpu.make_async_copy(vel, V.at[:, pl.ds(1, nx)], load_sem.at[0]),
        pltpu.make_async_copy(vis, Nu.at[:, pl.ds(1, nx)], load_sem.at[1]),
        pltpu.make_async_copy(prs, Pr.at[pl.ds(0, nx)], load_sem.at[2]),
        pltpu.make_async_copy(frc, F, load_sem.at[3]),
        pltpu.make_async_copy(src, S, load_sem.at[4]),
    ]
    for copy in loads:
        copy.start()

    barrier = pltpu.get_barrier_semaphore()
    for axis, index in (("gx", xu), ("gx", xd), ("gy", yu), ("gy", yd)):
        pl.semaphore_signal(barrier, inc=1, device_id={axis: index}, device_id_type=MESH)

    @pl.when(has_next)
    def _():
        pl.semaphore_signal(barrier, inc=1, device_id={"ta": t_next}, device_id_type=MESH)

    @pl.when(has_prev)
    def _():
        pl.semaphore_signal(barrier, inc=1, device_id={"ta": t_prev}, device_id_type=MESH)

    def remote(k, source, target, axis, index):
        return pltpu.make_async_remote_copy(
            src_ref=source, dst_ref=target, send_sem=send_sem.at[k], recv_sem=recv_sem.at[k],
            device_id={axis: index}, device_id_type=MESH,
        )

    vx_up = remote(0, V.at[:, nx], V.at[:, 0], "gx", xu)
    vx_dn = remote(1, V.at[:, 1], V.at[:, nx + 1], "gx", xd)
    px_dn = remote(2, Pr.at[0], Pr.at[nx], "gx", xd)
    nx_up = remote(3, Nu.at[0, nx], Nu.at[0, 0], "gx", xu)
    ry_up = remote(4, yu_s, yu_r, "gy", yu)
    ry_dn = remote(5, yd_s, yd_r, "gy", yd)
    fx_up = remote(6, W.at[0, nx], W.at[0, 0], "gx", xu)
    fy_up = remote(7, f_s, f_r, "gy", yu)
    cx_dn = remote(8, c1.at[1], c1.at[nx + 1], "gx", xd)
    cx_up = remote(9, c1.at[nx], c1.at[0], "gx", xu)
    cy_dn = remote(10, c1d_s, c1d_r, "gy", yd)
    cy_up = remote(11, c1u_s, c1u_r, "gy", yu)
    ex_dn = remote(12, c2x_s, c2.at[nx], "gx", xd)
    ey_dn = remote(13, c2y_s, c2y_r, "gy", yd)
    edge = remote(14, sE.at[:, pl.ds(2, nx - 2)], rE.at[:, pl.ds(2, nx - 2)], "ta", t_next)
    planes = remote(16, vel.at[:, pl.ds(0, 2)], rX, "ta", t_next)
    fe_up = remote(17 + len(groups), W.at[0, nx], fe_r, "gx", xu)
    border = remote(15, yu_r.at[1], rP, "ta", t_next)
    pieces = [
        remote(17 + k, sI.at[pl.ds(a, b - a)], rI.at[pl.ds(a, b - a)], "ta", t_next)
        for k, (a, b) in enumerate(groups)
    ]

    def pack_edges(x):
        for c in range(3):
            sE[c, x, 0:2] = V[c, x + 1, 0:2]
            sE[c, x, 2:4] = V[c, x + 1, ny - 2 : ny]

    def pack_rows(x):
        for c in range(3):
            yu_s[c, x] = V[c, x + 1, ny - 1 : ny]
            yd_s[c, x] = V[c, x + 1, 0:1]
        yu_s[3, x] = Nu[1, x + 1, ny - 1 : ny]
        yd_s[3, x] = Pr[x, 0:1]

    def pack_inner(x):
        for c in range(3):
            for p in range(parts):
                sI[x, p, c] = V[c, x + 1, 2 + 4 * p : 6 + 4 * p]

    pl.semaphore_wait(barrier, 4 + has_next.astype(jnp.int32) + has_prev.astype(jnp.int32))

    @pl.when(has_next)
    def _():
        planes.start()

    loads[0].wait()
    loop(2, nx, pack_edges)

    @pl.when(has_next)
    def _():
        edge.start()

    loads[1].wait()
    loads[2].wait()
    loop(0, nx, pack_rows)
    for copy in (ry_up, ry_dn, vx_up, vx_dn, px_dn, nx_up):
        copy.start()

    def coeff_of(nu):
        return 1.0 / (relax_factor * (1.0 + 6.0 * nu))

    loads[3].wait()
    vx_up.wait_recv()
    vx_dn.wait_recv()

    def pack_flux(x):
        e, j = x + 1, ny - 1
        v, nu = V[1, e, j:ny], Nu[1, e, j:ny]
        near = V[1, e - 1, j:ny] + V[1, e + 1, j:ny] + V[1, e, j - 1 : j] + z_last(v) + z_next(v)
        momentum = F[1, x, j:ny] - (v + nu * (6.0 * v - near)) + Pr[x, j:ny]
        f_s[x] = v + coeff_of(nu) * momentum

    loop(0, nx, pack_flux)
    fy_up.start()
    loop(2, nx, pack_inner)
    ry_up.wait_recv()

    @pl.when(has_next)
    def _():
        for copy in (border, *pieces):
            copy.start()

    loads[4].wait()
    for copy in (px_dn, nx_up, ry_dn):
        copy.wait_recv()
    C[0, 0] = coeff_of(Nu[0, 0])

    def prepare(x):
        e = x + 1
        below = coeff_of(yu_r[3, x])
        Ch[x] = below
        coeff = [coeff_of(Nu[c, e]) for c in range(3)]
        for c in range(3):
            C[c, e] = coeff[c]
        total = coeff[0] + C[0, x] + coeff[1] + y_last(coeff[1], below) + coeff[2] + z_last(coeff[2])
        SC[x] = damping / total
        press = Pr[x]
        grads = (Pr[x + 1] - press, y_next(press, yd_r[3, x]) - press, z_next(press) - press)
        for c in range(3):
            v = V[c, e]
            near = V[c, e - 1] + V[c, e + 1] + y_last(v, yu_r[c, x]) + y_next(v, yd_r[c, x])
            near = near + z_last(v) + z_next(v)
            momentum = F[c, x] - (v + Nu[c, e] * (6.0 * v - near)) - grads[c]
            W[c, e] = v + coeff[c] * momentum

    loop(0, nx, prepare)

    def add_edges(x):
        for c in range(3):
            for s, t in ((0, 0), (2, ny - 2)):
                W[c, x + 1, t : t + 2] = (
                    W[c, x + 1, t : t + 2] + C[c, x + 1, t : t + 2] * rE[c, x, s : s + 2]
                )

    def add_inner(x):
        for c in range(3):
            for p in range(parts):
                t = 2 + 4 * p
                W[c, x + 1, t : t + 4] = W[c, x + 1, t : t + 4] + C[c, x + 1, t : t + 4] * rI[x, p, c]

    def arrive(k):
        @pl.when(has_prev)
        def _():
            pieces[k].wait_recv()
            loop(*groups[k], add_inner)

    @pl.when(has_prev)
    def _():
        planes.wait_recv()
        for c in range(3):
            W[c, 1:3] = W[c, 1:3] + C[c, 1:3] * rX[c]
        edge.wait_recv()
        loop(2, nx, add_edges)

    fe_up.start()
    fy_up.wait_recv()

    def close_flux(x):
        Fh[x] = f_r[x] + Ch[x] * (yu_r[3, x] * V[1, x + 1, 0:1] - Pr[x, 0:1])

    loop(0, nx, close_flux)

    @pl.when(has_prev)
    def _():
        border.wait_recv()
        Fh[...] = Fh[...] + Ch[...] * rP[...]

    fe_up.wait_recv()

    def sweep_one(x, w0_last=None):
        e = x + 1
        w1, w2 = W[1, e], W[2, e]
        div = (W[0, e] - (W[0, x] if w0_last is None else w0_last)) + (w1 - y_last(w1, Fh[x])) + (w2 - z_last(w2))
        return SC[x] * (S[x] - div)

    def first(x):
        c1[x + 1] = sweep_one(x)

    def first_edges(x, w0_last=None):
        change = sweep_one(x, w0_last)
        c1[x + 1] = change
        c1d_s[x] = change[0:1]
        c1u_s[x] = change[ny - 1 : ny]

    first_edges(0, fe_r[...])
    loop(1, nx, first_edges)
    cy_dn.start()
    cy_up.start()
    fe_up.wait_send()
    arrive(0)
    fx_up.start()
    first(nx - 1)
    cx_up.start()
    fx_up.wait_recv()
    first(0)
    cx_dn.start()
    for copy in (cx_dn, cx_up, cy_dn, cy_up):
        copy.wait_recv()

    def sweep_two(x):
        e = x + 1
        here = c1[e]
        w0 = W[0, e] - C[0, e] * (c1[e + 1] - here)
        w0_last = W[0, x] - C[0, x] * (here - c1[x])
        w1 = W[1, e] - C[1, e] * (y_next(here, c1d_r[x]) - here)
        row = Fh[x] - Ch[x] * (here[0:1] - c1u_r[x])
        w2 = W[2, e] - C[2, e] * (z_next(here) - here)
        div = (w0 - w0_last) + (w1 - y_last(w1, row)) + (w2 - z_last(w2))
        return here + SC[x] * (S[x] - div)

    c2x_s[...] = sweep_two(0)

    def second_edges(x):
        c2y_s[x] = sweep_two(x)[0:1]

    loop(0, nx, second_edges)
    ey_dn.start()
    ex_dn.start()

    for copy in (cx_dn, cx_up):
        copy.wait_send()

    def second(x):
        c2[x] = sweep_two(x)

    def finish(x):
        e = x + 1
        here = c2[x]
        out_p[x] = Pr[x] + here
        out_v[0, x] = W[0, e] - C[0, e] * (c2[x + 1] - here)
        out_v[1, x] = W[1, e] - C[1, e] * (y_next(here, c2y_r[x]) - here)
        out_v[2, x] = W[2, e] - C[2, e] * (z_next(here) - here)

    def emit(a, b):
        loop(a, b, finish)

    done = 0
    for k in range(1, len(groups)):
        last = k == len(groups) - 1
        if last:
            ex_dn.wait_recv()
            ey_dn.wait_recv()
            ready = done - 2
            emit(0, ready)
        arrive(k)
        stop = nx if last else groups[k][1]
        loop(done, stop, first)
        loop(max(done - 1, 0), nx if last else stop - 1, second)
        done = stop
    emit(ready, nx)

    @pl.when(has_next)
    def _():
        planes.wait_send()
        edge.wait_send()
        border.wait_send()
        for copy in pieces:
            copy.wait_send()

    for copy in (vx_up, vx_dn, px_dn, nx_up, ry_up, ry_dn, fx_up, fy_up, cy_dn, cy_up, ex_dn, ey_dn):
        copy.wait_send()


def place(from_v, from_p, out_v, out_p, sem):
    copies = [
        pltpu.make_async_copy(from_v.at[c], out_v.at[c], sem.at[c]) for c in range(3)
    ] + [pltpu.make_async_copy(from_p, out_p, sem.at[3])]
    for copy in copies:
        copy.start()
    for copy in copies:
        copy.wait()


def body(counts, velocity, pressure, forcing, source, viscosity):
    _, steps, nx, ny, nz = velocity.shape
    assert steps == 1 and nx >= 8 and ny >= 8 and ny % 4 == 0
    groups = [(nx - 2, nx)] + groups_of(2, nx - 4, 5) + [(nx - 4, nx - 2)]
    parts = (ny - 4) // 4
    vmem = lambda *shape: pltpu.VMEM(shape, jnp.float32)
    rows = lambda *lead: vmem(*lead, nx, 1, nz)
    any_space = pl.BlockSpec(memory_space=pl.ANY)
    out_v, out_p = pl.pallas_call(
        functools.partial(kernel, *counts, groups),
        out_shape=(
            jax.ShapeDtypeStruct((3, nx, ny, nz), jnp.float32),
            jax.ShapeDtypeStruct((nx, ny, nz), jnp.float32),
        ),
        in_specs=[any_space] * 5,
        out_specs=(pl.BlockSpec(memory_space=pltpu.VMEM),) * 2,
        scratch_shapes=[
            vmem(3, nx + 2, ny, nz), vmem(nx + 1, ny, nz), vmem(3, nx, ny, nz), vmem(nx, ny, nz),
            vmem(3, nx + 1, ny, nz), vmem(3, nx + 1, ny, nz), vmem(3, nx + 1, ny, nz),
            vmem(nx, ny, nz), vmem(nx + 2, ny, nz), vmem(nx + 1, ny, nz),
            vmem(3, nx, 4, nz), vmem(3, nx, 4, nz),
            vmem(nx, parts, 3, 4, nz), vmem(nx, parts, 3, 4, nz),
            rows(4), rows(4), rows(4), rows(4), rows(), rows(), rows(), rows(), rows(), vmem(3, 2, ny, nz), vmem(ny, nz),
            rows(), rows(), rows(), rows(), vmem(ny, nz), rows(), rows(),
            pltpu.SemaphoreType.DMA((5,)),
            pltpu.SemaphoreType.DMA((18 + len(groups),)),
            pltpu.SemaphoreType.DMA((18 + len(groups),)),
        ],
        compiler_params=pltpu.CompilerParams(
            collective_id=0, has_side_effects=True, vmem_limit_bytes=48 << 20
        ),
        name="smoother",
    )(*(pltpu.with_memory_space_constraint(a, pltpu.HBM) for a in (velocity[:, 0], pressure[0], forcing[:, 0], source[0], viscosity)))
    out_v, out_p = pl.pallas_call(
        place,
        out_shape=(
            jax.ShapeDtypeStruct(out_v.shape, jnp.float32),
            jax.ShapeDtypeStruct(out_p.shape, jnp.float32),
        ),
        in_specs=[any_space] * 2,
        out_specs=(any_space, any_space),
        scratch_shapes=[pltpu.SemaphoreType.DMA((4,))],
        compiler_params=pltpu.CompilerParams(vmem_limit_bytes=1 << 20),
        name="place",
    )(out_v, out_p)
    return out_v[:, None], out_p[None]


def solution(mesh):
    placed = (
        P(None, "ta", "gx", "gy", None),
        P("ta", "gx", "gy", None),
        P(None, "ta", "gx", "gy", None),
        P("ta", "gx", "gy", None),
        P(None, "gx", "gy", None),
    )
    counts = tuple(mesh.shape[axis] for axis in ("ta", "gx", "gy"))
    return jax.shard_map(
        functools.partial(body, counts),
        mesh=mesh,
        in_specs=placed,
        out_specs=(P(None, "ta", "gx", "gy", None), P("ta", "gx", "gy", None)),
        check_vma=False,
    )
```
